32 devices in a mesh: dp: 8 (over y, x, core), tensor: 4 (over z).
Axes of the slice: x: 2, y: 2, z: 4, core: 2. Of those that a mesh axis runs over, the one named last changes fastest.
Arguments:
- hidden_in: bfloat16 [16384, 1024], P(('dp', 'tensor')), may hold values from -6 to 6
- value_first: bfloat16 [16384, 1024], P('dp', 'tensor'), may hold values from -6 to 6
- segment_ids: int32 [16384], P('dp'), may hold values from 0 to 8, as said below
- gain_attn: float32 [1024], replicated, may hold values from 0.25 to 1.75
- w_query: bfloat16 [1024, 1024], P('dp', 'tensor'), may hold values from -0.1875 to 0.1875
- w_key: bfloat16 [1024, 1024], P('dp', 'tensor'), may hold values from -0.1875 to 0.1875
- w_value: bfloat16 [1024, 1024], P('dp', 'tensor'), may hold values from -0.1875 to 0.1875
- w_out: bfloat16 [1024, 1024], P('tensor', 'dp'), may hold values from -3 to 3
- gain_ffn: float32 [1024], replicated, may hold values from 0.25 to 1.75
- w_gate: bfloat16 [1024, 2816], P('dp', 'tensor'), may hold values from -0.1875 to 0.1875
- w_up: bfloat16 [1024, 2816], P('dp', 'tensor'), may hold values from -0.1875 to 0.1875
- w_down: bfloat16 [2816, 1024], P('tensor', 'dp'), may hold values from -0.109375 to 0.109375
- cotangent: bfloat16 [16384, 1024], P(('dp', 'tensor')), may hold values from -6 to 6
Outputs:
- output: bfloat16 [16384, 1024], P(('dp', 'tensor'))
- grad_input: float32 [16384, 1024], P(('dp', 'tensor'))
- grad_value_first: float32 [16384, 1024], P('dp', 'tensor')
- grad_gain_attn: float32 [1024], P(('dp', 'tensor'))
- grad_w_query: float32 [1024, 1024], P('dp', 'tensor')
- grad_w_key: float32 [1024, 1024], P('dp', 'tensor')
- grad_w_value: float32 [1024, 1024], P('dp', 'tensor')
- grad_w_out: float32 [1024, 1024], P('tensor', 'dp')
- grad_gain_ffn: float32 [1024], P(('dp', 'tensor'))
- grad_w_gate: float32 [1024, 2816], P('dp', 'tensor')
- grad_w_up: float32 [1024, 2816], P('dp', 'tensor')
- grad_w_down: float32 [2816, 1024], P('tensor', 'dp')
The draws below stay inside these ranges and needn't reach their ends.
Inputs may be any that keep to these rules, and one draw needn't show every extreme that they name: `segment_ids`: in each group of 2048 tokens the first 1024 have id 0; then come continuations 1 to 8 in order, each of 64 to 192 tokens, and in every group one of them has exactly 192.
All inputs are finite; a program needn't handle non-finite values.
Results may differ from the reference program's by a relative error of at most 0.02.
Values may be sent and summed in bfloat16 or wider, within the bound.
No kernel may reach another device: no remote copies, remote signals or barrier semaphores. Data moves between devices by JAX's collectives and lax.ppermute only.
A program may use at most 192 MiB of HBM per device.

```python
import math
import jax
import jax.numpy as jnp
from jax import lax

D = 1024
HEADS = 16
HEAD_DIM = 64
FF = 2816
PROMPT_LEN = 1024
CONT_LEN = 128
CONTS = 8
GROUP_LEN = 2048
GROUPS = 8
TOKENS = 16384


def draw_segment_ids(key, part):
    pair_count = CONTS // 2
    key_size, key_sign = jax.random.split(key)
    offset = jax.random.randint(key_size, (GROUPS, pair_count), 0, CONT_LEN // 2 + 1).astype(jnp.int32)
    offset = offset.at[:, 0].set(CONT_LEN // 2)
    direction = 2 * jax.random.randint(key_sign, (GROUPS, pair_count), 0, 2).astype(jnp.int32) - 1
    moved = offset * direction
    lengths = jnp.stack([CONT_LEN + moved, CONT_LEN - moved], axis=2).reshape(GROUPS, CONTS)
    segment_ends = PROMPT_LEN + jnp.cumsum(lengths, axis=1)
    token_index = jnp.arange(PROMPT_LEN + CONTS * CONT_LEN, dtype=jnp.int32)
    passed = (token_index[None, None, :] >= segment_ends[:, :CONTS - 1, None]).astype(jnp.int32)
    labels = (token_index[None, :] >= PROMPT_LEN).astype(jnp.int32) + jnp.sum(passed, axis=1)
    return labels.reshape(-1).astype(jnp.int32)


def with_spikes(entries, stream_key, source, target, blocks, factor):
    owner, partner = [(jnp.arange(entries.shape[dim]) // (entries.shape[dim] // blocks)).reshape([-1 if axis == dim else 1 for axis in range(entries.ndim)]) for dim in (source, target)]
    chosen = jax.random.permutation(stream_key, blocks)[partner]
    strong = (owner == chosen) | (owner == (partner + blocks // 2) % blocks)
    return jnp.where(strong, factor * entries, entries)


def block_levels(rng, shape, shards, low, largest):
    level = 1.0
    for dim, shards_of in shards:
        draws = jax.random.uniform(jax.random.fold_in(jax.random.fold_in(rng, 6), dim), (shards_of,), jnp.float32, low / len(shards), largest / len(shards))
        level = level * jnp.repeat(jnp.exp(draws), shape[dim] // shards_of).reshape((-1,) + (1,) * (len(shape) - 1 - dim))
    return level


def scatter_about(own_key, dims, width, limit, cuts=(), held_as=jnp.bfloat16):
    entries = jax.random.normal(own_key, dims, jnp.float32) * width
    if len(cuts) > 0:
        entries = block_levels(own_key, dims, cuts, -0.22, 0.18) * entries
    return jnp.clip(entries, min=-limit, max=limit).astype(held_as)


def bell_draw_with(own_key, shape, width, reach, pieces, heavy, kind=jnp.bfloat16):
    values = width * jax.random.normal(own_key, shape, jnp.float32)
    if pieces:
        values = values * block_levels(own_key, shape, pieces, -0.22, 0.18)
    return jnp.clip(with_spikes(values, jax.random.fold_in(own_key, 3), *heavy), -reach, reach).astype(kind)


def setup_inputs(seed: int = 0) -> dict:
    seeds = jax.random.split(jax.random.key(seed), 14)
    hidden_in = scatter_about(seeds[0], (TOKENS, D), 1.0, 6.0, ((0, 32),))
    value_first = scatter_about(seeds[1], (TOKENS, D), 1.0, 6.0, ((0, 8), (1, 4)))
    segment_ids = draw_segment_ids(jax.random.fold_in(seeds[13], 71), 0)
    gain_attn = jnp.clip(1.0 + 0.15 * jax.random.normal(seeds[3], (D,), jnp.float32), 0.25, 1.75)
    w_query = scatter_about(seeds[4], (D, D), D ** -0.5, 0.1875, ((0, 8), (1, 4)))
    w_key = scatter_about(seeds[5], (D, D), D ** -0.5, 0.1875, ((0, 8), (1, 4)))
    w_value = scatter_about(seeds[6], (D, D), D ** -0.5, 0.1875, ((0, 8), (1, 4)))
    w_out = scatter_about(seeds[7], (D, D), (max(D // 256, 1)) ** -0.5, 3.0, ((0, 4), (1, 8)))
    gain_ffn = jnp.clip(1.0 + 0.15 * jax.random.normal(seeds[8], (D,), jnp.float32), 0.25, 1.75)
    w_gate = scatter_about(seeds[9], (D, FF), D ** -0.5, 0.1875, ((0, 8), (1, 4)))
    w_up = scatter_about(seeds[10], (D, FF), D ** -0.5, 0.1875, ((0, 8), (1, 4)))
    w_down = scatter_about(seeds[11], (FF, D), FF ** -0.5, 0.109375, ((0, 4), (1, 8)))
    cotangent = bell_draw_with(seeds[12], (TOKENS, D), 1.0, 6.0, ((0, 32),), (0, 1, 32, 2.75))
    return {"hidden_in": hidden_in, "value_first": value_first, "segment_ids": segment_ids, "gain_attn": gain_attn, "w_query": w_query, "w_key": w_key, "w_value": w_value, "w_out": w_out, "gain_ffn": gain_ffn, "w_gate": w_gate, "w_up": w_up, "w_down": w_down, "cotangent": cotangent}


@jax.custom_vjp
def low(v):
    return lax.optimization_barrier(v.astype(jnp.bfloat16)).astype(jnp.float32)

@jax.custom_vjp
def low_back(v):
    return v

def low_keep(v):
    return (low(v), None)

def low_pass(kept, grad):
    return (grad,)

def back_keep(v):
    return (v, None)

def back_low(kept, grad):
    return (low(grad),)
low.defvjp(low_keep, low_pass)
low_back.defvjp(back_keep, back_low)
epsilon = 1e-06
highest = lax.Precision.HIGHEST

def block_rows(total_rows):
    block_size = min(512, total_rows)
    while total_rows % block_size:
        block_size = block_size + 1
    return block_size

def token_positions(segment):
    token_index = jnp.arange(segment.shape[0], dtype=jnp.int32)
    change = jnp.concatenate([jnp.ones((1,), dtype=jnp.bool_), segment[1:] != segment[:-1]])
    starts = lax.cummax(jnp.where(change, token_index, 0).astype(jnp.int32), axis=0)
    return (token_index - starts + PROMPT_LEN * (segment > 0).astype(jnp.int32)).astype(jnp.int32)

def rotation_tables(position):
    half_dim = HEAD_DIM // 2
    frequency = jnp.exp(jnp.arange(half_dim, dtype=jnp.float32) * (-2.0 * math.log(10000.0) / HEAD_DIM))
    phase_angle = position.astype(jnp.float32)[:, None] * frequency[None, :]
    return (jnp.cos(phase_angle), jnp.sin(phase_angle))

def rotate(field, cosine, sine):
    row_count = field.shape[0]
    halves = field.reshape(row_count, -1, 2, HEAD_DIM // 2)
    first_half = halves[:, :, 0, :]
    second_half = halves[:, :, 1, :]
    cos_rows = cosine[:, None, :]
    sin_rows = sine[:, None, :]
    turned = jnp.stack([first_half * cos_rows - second_half * sin_rows, second_half * cos_rows + first_half * sin_rows], axis=2)
    return turned.reshape(row_count, -1)

def rms_scale(rows_in, gain_vector):
    return rows_in * lax.rsqrt(lax.optimization_barrier(jnp.mean(rows_in * rows_in, axis=-1, keepdims=True)) + epsilon) * gain_vector

def group_attention(group_inputs):
    query_rot, key_rot, value_mix, segment, position = group_inputs
    group_len = query_rot.shape[0]
    block_size = block_rows(group_len)
    key_heads = key_rot.reshape(group_len, HEADS, HEAD_DIM)
    value_heads = value_mix.reshape(group_len, HEADS, HEAD_DIM)

    def one_block(block_inputs):
        query_block, segment_block, position_block = block_inputs
        query_heads = query_block.reshape(block_size, HEADS, HEAD_DIM)
        scores = jnp.einsum('qhd,khd->hqk', query_heads, key_heads, precision=highest) * 0.125
        visible = ((segment[None, :] == 0) | (segment[None, :] == segment_block[:, None])) & (position[None, :] <= position_block[:, None])
        scores = low_back(jnp.where(visible[None], scores, -1e+30))
        row_top = lax.optimization_barrier(jnp.max(scores, axis=-1, keepdims=True))
        expo = jnp.exp(scores - row_top)
        weights = low(expo / lax.optimization_barrier(jnp.sum(expo, axis=-1, keepdims=True)))
        mixed_rows = jnp.einsum('hqk,khd->qhd', weights, value_heads, precision=highest)
        return mixed_rows.reshape(block_size, HEADS * HEAD_DIM)
    block_count = group_len // block_size
    outputs = lax.map(jax.checkpoint(one_block), (query_rot.reshape(block_count, block_size, -1), segment.reshape(block_count, block_size), position.reshape(block_count, block_size)))
    return outputs.reshape(group_len, -1)

def reference(hidden_in, value_first, segment_ids, gain_attn, w_query, w_key, w_value, w_out, gain_ffn, w_gate, w_up, w_down, cotangent):
    group_count = segment_ids.shape[0] // GROUP_LEN
    segment_groups = segment_ids.reshape(group_count, GROUP_LEN)
    position_groups = jax.vmap(token_positions)(segment_groups)
    cosine, sine = rotation_tables(position_groups.reshape(-1))

    def forward(hidden_rows, value_rows, gain_one, query_weight, key_weight, value_weight, out_weight, gain_two, gate_weight, up_weight, down_weight):
        normed_attn = low(rms_scale(hidden_rows, gain_one))
        query_proj = low_back(jnp.dot(normed_attn, query_weight, precision=highest, preferred_element_type=jnp.float32))
        key_proj = low_back(jnp.dot(normed_attn, key_weight, precision=highest, preferred_element_type=jnp.float32))
        value_proj = low_back(jnp.dot(normed_attn, value_weight, precision=highest, preferred_element_type=jnp.float32))
        query_rot = low(rotate(query_proj, cosine, sine))
        key_rot = low(rotate(key_proj, cosine, sine))
        value_mix = low(0.5 * value_proj + 0.5 * value_rows)
        attended = lax.map(group_attention, (query_rot.reshape(group_count, GROUP_LEN, -1), key_rot.reshape(group_count, GROUP_LEN, -1), value_mix.reshape(group_count, GROUP_LEN, -1), segment_groups, position_groups))
        attended = low_back(low(attended.reshape(-1, D)))
        middle = hidden_rows + low_back(jnp.dot(attended, out_weight, precision=highest, preferred_element_type=jnp.float32))
        normed_ffn = low(rms_scale(middle, gain_two))
        gate_act = low_back(jnp.dot(normed_ffn, gate_weight, precision=highest, preferred_element_type=jnp.float32))
        up_act = low_back(jnp.dot(normed_ffn, up_weight, precision=highest, preferred_element_type=jnp.float32))
        hidden_act = low(jax.nn.silu(gate_act) * up_act)
        return middle + low_back(jnp.dot(hidden_act, down_weight, precision=highest, preferred_element_type=jnp.float32))
    primals = (hidden_in.astype(jnp.float32), value_first.astype(jnp.float32), gain_attn.astype(jnp.float32), w_query.astype(jnp.float32), w_key.astype(jnp.float32), w_value.astype(jnp.float32), w_out.astype(jnp.float32), gain_ffn.astype(jnp.float32), w_gate.astype(jnp.float32), w_up.astype(jnp.float32), w_down.astype(jnp.float32))
    result, pullback = jax.vjp(forward, *primals)
    gradients = pullback(cotangent.astype(jnp.float32))
    return (result.astype(jnp.bfloat16), gradients[0], gradients[1], gradients[2], gradients[3], gradients[4], gradients[5], gradients[6], gradients[7], gradients[8], gradients[9], gradients[10])
```

```python
import functools
import math

import jax
import jax.numpy as jnp
from jax import lax
from jax.experimental import pallas as pl
from jax.experimental.pallas import tpu as pltpu
from jax.sharding import Mesh
from jax.sharding import PartitionSpec as P

HEAD_DIM = 64
PROMPT_LEN = 1024
BLOCK = 256
BF16 = jnp.bfloat16
F32 = jnp.float32
VMEM_LIMIT = 56 * 1024 * 1024

epsilon = 1e-06


def token_positions(segment):
    ids = jnp.arange(1, 9, dtype=jnp.int32)
    token_index = jnp.arange(segment.shape[0], dtype=jnp.int32)
    starts = jnp.sum((segment[None, :] < ids[:, None]).astype(jnp.int32), axis=1)
    own = jnp.sum(jnp.where(segment[None, :] == ids[:, None], starts[:, None], 0), axis=0)
    return token_index - own + PROMPT_LEN * (segment > 0).astype(jnp.int32)


def rotation_tables(position):
    half_dim = HEAD_DIM // 2
    frequency = jnp.exp(
        jnp.arange(half_dim, dtype=F32) * (-2.0 * math.log(10000.0) / HEAD_DIM)
    )
    angle = position.astype(F32)[:, None] * frequency[None, :]
    cosine, sine = jnp.cos(angle), jnp.sin(angle)
    return (
        jnp.concatenate([cosine] * 4, axis=1),
        jnp.concatenate([-sine, sine] * 2, axis=1),
    )


def contract_rows(left, right):
    return lax.dot_general(left, right, (((0,), (0,)), ((), ())), preferred_element_type=F32)


def contract_cols(left, right):
    return lax.dot_general(left, right, (((1,), (1,)), ((), ())), preferred_element_type=F32)


def matmul(left, right):
    return jnp.dot(left, right, preferred_element_type=F32)


def turn(field, cosine, sine):
    lane = lax.broadcasted_iota(jnp.int32, cosine.shape, 1)
    first = (lane % HEAD_DIM) < HEAD_DIM // 2
    parts = []
    for start in range(0, field.shape[1], 128):
        part = field[:, start : start + 128]
        partner = jnp.where(first, pltpu.roll(part, 96, 1), pltpu.roll(part, 32, 1))
        parts.append(part * cosine + partner * sine)
    return jnp.concatenate(parts, axis=1)


def project_kernel(
    blk_ref, x_ref, w_ref, gain_ref, cos_ref, sin_ref, first_ref, *rest
):
    n_ref, q_ref, k_ref, v_ref = rest[-4:]
    x = x_ref[...].astype(F32)
    inverse = lax.rsqrt(jnp.mean(x * x, axis=1, keepdims=True) + epsilon)
    normed = (x * inverse * gain_ref[...]).astype(BF16)
    n_ref[...] = normed
    width = q_ref.shape[1]
    cosine, sine = cos_ref[...], sin_ref[...]
    q_ref[...] = turn(matmul(normed, w_ref[:, :width]), cosine, sine).astype(BF16)
    k_ref[...] = turn(matmul(normed, w_ref[:, width : 2 * width]), cosine, sine).astype(BF16)
    v_ref[...] = (
        0.5 * matmul(normed, w_ref[:, 2 * width :]) + 0.5 * first_ref[...].astype(F32)
    ).astype(BF16)


def project(block, before, x_part, w_qkv, gain, cosine, sine, value_first):
    rows, model = x_part.shape
    tokens, width = value_first.shape
    row = lambda cols: pl.BlockSpec((rows, cols), lambda i, b: (b[0], 0))
    whole = lambda shape: pl.BlockSpec(shape, lambda i, b: (0, 0))
    return pl.pallas_call(
        project_kernel,
        grid_spec=pltpu.PrefetchScalarGridSpec(
            num_scalar_prefetch=1,
            grid=(1,),
            in_specs=[
                whole((rows, model)), whole(w_qkv.shape), whole((1, model)),
                row(128), row(128), row(width),
            ] + [pl.BlockSpec(memory_space=pl.ANY)] * len(before),
            out_specs=[row(model), row(width), row(width), row(width)],
        ),
        out_shape=[jax.ShapeDtypeStruct((tokens, model), BF16)]
        + [jax.ShapeDtypeStruct((tokens, width), BF16)] * 3,
        input_output_aliases={7 + i: i for i in range(len(before))},
        compiler_params=pltpu.CompilerParams(vmem_limit_bytes=VMEM_LIMIT),
        cost_estimate=pl.CostEstimate(
            flops=2 * rows * model * 3 * width, bytes_accessed=5 << 20, transcendentals=0
        ),
        name="project",
    )(block, x_part, w_qkv, gain, cosine, sine, value_first, *before)


def unproject_kernel(final, blk_ref, g_ref, w_ref, x_ref, gain_ref, *rest):
    part = contract_cols(g_ref[...], w_ref[...])
    x = x_ref[...].astype(F32)
    inverse = lax.rsqrt(jnp.mean(x * x, axis=1, keepdims=True) + epsilon)
    scaled = x * inverse
    rest[-1][...] = jnp.sum(part * scaled, axis=0, keepdims=True)
    if len(rest) > 2:
        part = part + rest[0][...].astype(F32)
    if not final:
        rest[-2][...] = part.astype(BF16)
        return
    weighted = part * gain_ref[...]
    rest[-2][...] = rest[1][...] + inverse * (
        weighted - scaled * jnp.mean(weighted * scaled, axis=1, keepdims=True)
    )


def unproject(block, qkv_grads, w_qkv, x_part, gain, arrived, grad_middle):
    rows, model = x_part.shape
    final = grad_middle is not None
    whole = lambda shape: pl.BlockSpec(shape, lambda i, b: (0, 0))
    more = [v for v in (arrived, grad_middle) if v is not None]
    return pl.pallas_call(
        functools.partial(unproject_kernel, final),
        grid_spec=pltpu.PrefetchScalarGridSpec(
            num_scalar_prefetch=1,
            grid=(1,),
            in_specs=[
                pl.BlockSpec((rows, qkv_grads.shape[1]), lambda i, b: (b[0], 0)),
                whole(w_qkv.shape), whole((rows, model)), whole((1, model)),
            ] + [whole((rows, model))] * len(more),
            out_specs=[whole((rows, model)), whole((1, model))],
        ),
        out_shape=[
            jax.ShapeDtypeStruct((rows, model), F32 if final else BF16),
            jax.ShapeDtypeStruct((1, model), F32),
        ],
        compiler_params=pltpu.CompilerParams(vmem_limit_bytes=VMEM_LIMIT),
        cost_estimate=pl.CostEstimate(
            flops=2 * rows * model * qkv_grads.shape[1], bytes_accessed=5 << 20, transcendentals=0
        ),
        name="unproject",
    )(block, qkv_grads, w_qkv, x_part, gain, *more)


def head_lanes(width, head):
    lane = lax.broadcasted_iota(jnp.int32, (1, width), 1)
    return (lane // HEAD_DIM) == head


def attend_kernel(q_ref, k_ref, v_ref, segc_ref, segr_ref, o_ref, lse_ref, qh_ref, acc_ref):
    head = pl.program_id(0)
    tokens, width = q_ref.shape
    keep = head_lanes(width, head)
    keep_low = jnp.where(keep, 0.125, 0.0).astype(BF16)
    qh_ref[...] = q_ref[...] * keep_low
    prompt_blocks = PROMPT_LEN // BLOCK

    @pl.when(head == 0)
    def _():
        acc_ref[...] = jnp.zeros_like(acc_ref)

    for qi in range(tokens // BLOCK):
        q0 = qi * BLOCK
        query = qh_ref[q0 : q0 + BLOCK, :]
        plain = qi if qi < prompt_blocks else prompt_blocks
        first_masked = qi if qi <= prompt_blocks else qi - 1
        row_ids = q0 + lax.broadcasted_iota(jnp.int32, (BLOCK, 1), 0)
        scores, tops = [], []
        if plain:
            s = contract_cols(query, k_ref[: plain * BLOCK, :])
            scores.append((s, 0))
            tops.append(jnp.max(s, axis=1, keepdims=True))
        k0, k1 = first_masked * BLOCK, (qi + 1) * BLOCK
        s = contract_cols(query, k_ref[k0:k1, :])
        col_ids = k0 + lax.broadcasted_iota(jnp.int32, (1, k1 - k0), 1)
        visible = col_ids <= row_ids
        if qi >= prompt_blocks:
            visible = visible & (segc_ref[q0 : q0 + BLOCK, :] == segr_ref[:, k0:k1])
        s = jnp.where(visible, s, -1e30)
        scores.append((s, k0))
        tops.append(jnp.max(s, axis=1, keepdims=True))
        top = functools.reduce(jnp.maximum, tops)
        total, mixed = None, None
        for s, start in scores:
            p = jnp.exp(s - top)
            part = jnp.sum(p, axis=1, keepdims=True)
            total = part if total is None else total + part
            part = matmul(p.astype(BF16), v_ref[start : start + s.shape[1], :])
            mixed = part if mixed is None else mixed + part
        acc_ref[q0 : q0 + BLOCK, :] = jnp.where(
            keep, mixed / total, acc_ref[q0 : q0 + BLOCK, :]
        )
        lse = top + jnp.log(total)
        lse_ref[:, q0 : q0 + BLOCK] = jnp.broadcast_to(lse, (BLOCK, 128)).T[0:1, :]

    @pl.when(head == pl.num_programs(0) - 1)
    def _():
        o_ref[...] = acc_ref[...].astype(BF16)


def attend(query, key, value, seg_col, seg_row):
    tokens, width = query.shape
    heads = width // HEAD_DIM
    whole = lambda shape: pl.BlockSpec(shape, lambda h: (0, 0))
    return pl.pallas_call(
        attend_kernel,
        grid=(heads,),
        in_specs=[whole((tokens, width))] * 3 + [whole((tokens, 1)), whole((1, tokens))],
        out_specs=[
            whole((tokens, width)),
            pl.BlockSpec((pl.Squeezed(), 1, tokens), lambda h: (h, 0, 0)),
        ],
        out_shape=[
            jax.ShapeDtypeStruct((tokens, width), BF16),
            jax.ShapeDtypeStruct((heads, 1, tokens), F32),
        ],
        scratch_shapes=[pltpu.VMEM((tokens, width), BF16), pltpu.VMEM((tokens, width), F32)],
        compiler_params=pltpu.CompilerParams(vmem_limit_bytes=VMEM_LIMIT),
        cost_estimate=pl.CostEstimate(
            flops=9 << 30, bytes_accessed=8 << 20, transcendentals=9 << 20
        ),
        name="attend",
    )(query, key, value, seg_col, seg_row)


def attend_back_kernel(
    q_ref, k_ref, v_ref, do_ref, o_ref, lse_ref, segc_ref, segr_ref, cos_ref, sin_ref,
    grads_ref, first_ref, qh_ref, kh_ref, doh_ref, dq_ref, dk_ref, dv_ref,
):
    head = pl.program_id(0)
    tokens, width = q_ref.shape
    keep = jnp.where(head_lanes(width, head), 1.0, 0.0)
    keep_low = keep.astype(BF16)
    qh_ref[...] = q_ref[...] * (0.125 * keep).astype(BF16)
    kh_ref[...] = k_ref[...] * keep_low
    doh_ref[...] = do_ref[...] * keep_low
    prompt_blocks = PROMPT_LEN // BLOCK
    blocks = tokens // BLOCK

    @pl.when(head == 0)
    def _():
        dq_ref[...] = jnp.zeros_like(dq_ref)
        dk_ref[...] = jnp.zeros_like(dk_ref)
        dv_ref[...] = jnp.zeros_like(dv_ref)

    ones = jnp.ones((8, width), F32)
    deltas = []
    for qi in range(blocks):
        rows = slice(qi * BLOCK, (qi + 1) * BLOCK)
        product = o_ref[rows, :].astype(F32) * doh_ref[rows, :].astype(F32)
        deltas.append(
            lax.dot_general(
                ones, product, (((1,), (1,)), ((), ())),
                precision=lax.Precision.HIGHEST, preferred_element_type=F32,
            )[0:1, :]
        )

    for kj in range(blocks):
        k0 = kj * BLOCK
        keys = slice(k0, k0 + BLOCK)
        last = blocks if kj < prompt_blocks else min(kj + 2, blocks)
        key_ids = k0 + lax.broadcasted_iota(jnp.int32, (BLOCK, 1), 0)
        sum_k, sum_v = None, None
        for qi in range(kj, last):
            rows = slice(qi * BLOCK, (qi + 1) * BLOCK)
            s = contract_cols(k_ref[keys, :], qh_ref[rows, :])
            p = jnp.exp(s - lse_ref[:, rows])
            if qi == kj or kj >= prompt_blocks:
                query_ids = qi * BLOCK + lax.broadcasted_iota(jnp.int32, (1, BLOCK), 1)
                visible = key_ids <= query_ids
                if kj >= prompt_blocks:
                    visible = visible & (segc_ref[keys, :] == segr_ref[:, rows])
                p = jnp.where(visible, p, 0.0)
            dp = contract_cols(v_ref[keys, :], doh_ref[rows, :])
            ds = (p * (dp - deltas[qi])).astype(BF16)
            part_v = matmul(p.astype(BF16), doh_ref[rows, :])
            part_k = matmul(ds, qh_ref[rows, :])
            sum_v = part_v if sum_v is None else sum_v + part_v
            sum_k = part_k if sum_k is None else sum_k + part_k
            dq_ref[rows, :] += contract_rows(ds, kh_ref[keys, :])
        dk_ref[keys, :] += sum_k
        dv_ref[keys, :] += sum_v

    @pl.when(head == pl.num_programs(0) - 1)
    def _():
        for qi in range(blocks):
            rows = slice(qi * BLOCK, (qi + 1) * BLOCK)
            cosine, sine = cos_ref[rows, :], -sin_ref[rows, :]
            half_v = 0.5 * dv_ref[rows, :]
            first_ref[rows, :] = half_v
            grads_ref[rows, :width] = turn(0.125 * dq_ref[rows, :], cosine, sine).astype(BF16)
            grads_ref[rows, width : 2 * width] = turn(dk_ref[rows, :], cosine, sine).astype(BF16)
            grads_ref[rows, 2 * width :] = half_v.astype(BF16)


def attend_back(query, key, value, grad_out, out, lse, seg_col, seg_row, cosine, sine):
    tokens, width = query.shape
    heads = width // HEAD_DIM
    whole = lambda shape: pl.BlockSpec(shape, lambda h: (0, 0))
    wide = whole((tokens, width))
    return pl.pallas_call(
        attend_back_kernel,
        grid=(heads,),
        in_specs=[
            wide, wide, wide, wide, wide,
            pl.BlockSpec((pl.Squeezed(), 1, tokens), lambda h: (h, 0, 0)),
            whole((tokens, 1)), whole((1, tokens)), whole((tokens, 128)), whole((tokens, 128)),
        ],
        out_specs=[whole((tokens, 3 * width)), wide],
        out_shape=[
            jax.ShapeDtypeStruct((tokens, 3 * width), BF16),
            jax.ShapeDtypeStruct((tokens, width), F32),
        ],
        scratch_shapes=[pltpu.VMEM((tokens, width), BF16)] * 3
        + [pltpu.VMEM((tokens, width), F32)] * 3,
        compiler_params=pltpu.CompilerParams(vmem_limit_bytes=VMEM_LIMIT),
        cost_estimate=pl.CostEstimate(
            flops=22 << 30, bytes_accessed=14 << 20, transcendentals=9 << 20
        ),
        name="attend_back",
    )(query, key, value, grad_out, out, lse, seg_col, seg_row, cosine, sine)


def fill_out_kernel(at_ref, mine_ref, other_ref, full_ref):
    rings, pairs, rows, wide = mine_ref.shape
    core = at_ref[2]
    for ring in range(rings):
        head_row = lax.rem(at_ref[0] + rings - ring, rings) * (2 * rows)
        for pair in range(pairs):
            column = (at_ref[1] ^ pair) * wide
            for source, owner in ((mine_ref, core), (other_ref, 1 - core)):
                start = pl.multiple_of(column + owner * (wide // 2), wide // 2)
                for top in range(2):
                    row = pl.multiple_of(head_row + top * rows, rows)
                    full_ref[pl.ds(row, rows), pl.ds(start, wide // 2)] = source[
                        ring, pair, :, top * (wide // 2) : (top + 1) * (wide // 2)
                    ]


def fill_out(place, mine, other):
    rings, pairs, rows, wide = mine.shape
    return pl.pallas_call(
        fill_out_kernel,
        grid_spec=pltpu.PrefetchScalarGridSpec(
            num_scalar_prefetch=1,
            grid=(1,),
            in_specs=[pl.BlockSpec(mine.shape, lambda i, b: (0, 0, 0, 0))] * 2,
            out_specs=pl.BlockSpec((rings * rows * 2, pairs * wide), lambda i, b: (0, 0)),
        ),
        out_shape=jax.ShapeDtypeStruct((rings * rows * 2, pairs * wide), BF16),
        compiler_params=pltpu.CompilerParams(vmem_limit_bytes=VMEM_LIMIT),
        cost_estimate=pl.CostEstimate(flops=0, bytes_accessed=4 << 20, transcendentals=0),
        name="fill_out",
    )(place, mine, other)


def middle_kernel(a_ref, w_ref, x_ref, gain_ref, mid_ref, n_ref):
    middle = x_ref[...].astype(F32) + matmul(a_ref[...], w_ref[...])
    mid_ref[...] = middle
    inverse = lax.rsqrt(jnp.mean(middle * middle, axis=1, keepdims=True) + epsilon)
    n_ref[...] = (middle * inverse * gain_ref[...]).astype(BF16)


def middle_rows(attended, out_full, hidden_in, gain):
    rows, model = hidden_in.shape
    step = 256
    row = pl.BlockSpec((step, model), lambda i: (i, 0))
    return pl.pallas_call(
        middle_kernel,
        grid=(rows // step,),
        in_specs=[
            row, pl.BlockSpec(out_full.shape, lambda i: (0, 0)), row,
            pl.BlockSpec((1, model), lambda i: (0, 0)),
        ],
        out_specs=[row, row],
        out_shape=[
            jax.ShapeDtypeStruct((rows, model), F32), jax.ShapeDtypeStruct((rows, model), BF16),
        ],
        compiler_params=pltpu.CompilerParams(vmem_limit_bytes=VMEM_LIMIT),
        cost_estimate=pl.CostEstimate(
            flops=2 * rows * model * model, bytes_accessed=7 << 20, transcendentals=0
        ),
        name="middle",
    )(attended, out_full, hidden_in, gain)


def middle_back_kernel(d_ref, r_ref, mid_ref, c_ref, gain_ref, w_ref, gm_ref, low_ref, ga_ref, gg_ref):
    middle = mid_ref[...]
    inverse = lax.rsqrt(jnp.mean(middle * middle, axis=1, keepdims=True) + epsilon)
    scaled = middle * inverse
    grad = d_ref[...] + r_ref[...].astype(F32)
    part = jnp.sum(grad * scaled, axis=0, keepdims=True)

    @pl.when(pl.program_id(0) == 0)
    def _():
        gg_ref[...] = part

    @pl.when(pl.program_id(0) != 0)
    def _():
        gg_ref[...] += part

    weighted = grad * gain_ref[...]
    grad_middle = c_ref[...].astype(F32) + inverse * (
        weighted - scaled * jnp.mean(weighted * scaled, axis=1, keepdims=True)
    )
    gm_ref[...] = grad_middle
    low = grad_middle.astype(BF16)
    low_ref[...] = low
    ga_ref[...] = contract_cols(low, w_ref[...]).astype(BF16)


def middle_back(grad_own, arrived, middle, cotangent, gain, out_full):
    rows, model = middle.shape
    step = 256
    row = pl.BlockSpec((step, model), lambda i: (i, 0))
    one = pl.BlockSpec((1, model), lambda i: (0, 0))
    return pl.pallas_call(
        middle_back_kernel,
        grid=(rows // step,),
        in_specs=[row, row, row, row, one, pl.BlockSpec(out_full.shape, lambda i: (0, 0))],
        out_specs=[row, row, row, one],
        out_shape=[
            jax.ShapeDtypeStruct((rows, model), F32),
            jax.ShapeDtypeStruct((rows, model), BF16),
            jax.ShapeDtypeStruct((rows, out_full.shape[0]), BF16),
            jax.ShapeDtypeStruct((1, model), F32),
        ],
        compiler_params=pltpu.CompilerParams(vmem_limit_bytes=VMEM_LIMIT),
        cost_estimate=pl.CostEstimate(
            flops=2 * rows * model * model, bytes_accessed=12 << 20, transcendentals=0
        ),
        name="middle_back",
    )(grad_own, arrived, middle, cotangent, gain, out_full)


def block_copies(place_ref, blocks, target, sems, first_row, rows, pairs):
    wide = target.shape[1] // pairs
    copies = []
    for index, block in enumerate(blocks):
        ring, pair = divmod(index, pairs)
        start = 0 if pairs == 1 else pl.multiple_of((place_ref[1] ^ pair) * wide, wide)
        copies.append(
            pltpu.make_async_copy(
                block.at[pl.ds(first_row, rows), :],
                target.at[pl.ds(ring * rows, rows), pl.ds(start, wide)],
                sems.at[index],
            )
        )
    return copies


def ffn_kernel(pairs, half, place_ref, n0_ref, n1_ref, c0_ref, c1_ref, *rest):
    count = len(rest) - 9
    blocks = rest[:count]
    dx0_ref, dx1_ref, h_ref, ht_ref, gt_ref, ut_ref, full_ref, sems = rest[count : count + 8]
    step_id = pl.program_id(0)
    rows_of = rest[-1]
    order = (0, 1, 2)

    def copies(which):
        return block_copies(
            place_ref, blocks, full_ref.at[which], sems.at[which], which * half, half, pairs
        )

    @pl.when(step_id == 0)
    def _():
        for which in order:
            for copy in copies(which):
                copy.start()
        for which in order:
            for copy in copies(which):
                copy.wait()

    mine = step_id < pl.num_programs(0) // 2
    rows_of[0] = jnp.where(mine, n0_ref[...], n1_ref[...])
    rows_of[1] = jnp.where(mine, c0_ref[...], c1_ref[...])
    normed, cot = rows_of[0], rows_of[1]
    gate = contract_cols(normed, full_ref[0])
    up = contract_cols(normed, full_ref[1])
    grad = contract_cols(cot, full_ref[2])
    sig = jax.nn.sigmoid(gate)
    silu = gate * sig
    hidden = (silu * up).astype(BF16)
    grad_up = (grad * silu).astype(BF16)
    grad_gate = (grad * up * sig * (1.0 + gate * (1.0 - sig))).astype(BF16)
    h_ref[...] = hidden
    ht_ref[...] = hidden.T
    gt_ref[...] = grad_gate.T
    ut_ref[...] = grad_up.T
    dx = matmul(grad_gate, full_ref[0]) + matmul(grad_up, full_ref[1])

    @pl.when(mine)
    def _():
        dx0_ref[...] = dx

    @pl.when(jnp.logical_not(mine))
    def _():
        dx1_ref[...] = dx.astype(BF16)


def ffn(place, normed, normed_other, cot, cot_other, blocks, half, pairs):
    rows, model = normed.shape
    step = 256
    each = rows // step
    rings = len(blocks) // pairs
    units = half * rings
    own = pl.BlockSpec((step, model), lambda i, b: (jnp.minimum(i, each - 1), 0))
    other = pl.BlockSpec((step, model), lambda i, b: (jnp.maximum(i - each, 0), 0))
    turned = pl.BlockSpec((units, step), lambda i, b: (0, i))
    return pl.pallas_call(
        functools.partial(ffn_kernel, pairs, half),
        grid_spec=pltpu.PrefetchScalarGridSpec(
            num_scalar_prefetch=1,
            grid=(2 * each,),
            in_specs=[own, other, own, other]
            + [pl.BlockSpec(memory_space=pl.ANY)] * len(blocks),
            out_specs=[
                own, other, pl.BlockSpec((step, units), lambda i, b: (i, 0)),
                turned, turned, turned,
            ],
            scratch_shapes=[
                pltpu.VMEM((3, units, model), BF16),
                pltpu.SemaphoreType.DMA((3, len(blocks))),
                pltpu.VMEM((2, step, model), BF16),
            ],
        ),
        out_shape=[
            jax.ShapeDtypeStruct((rows, model), F32),
            jax.ShapeDtypeStruct((rows, model), BF16),
            jax.ShapeDtypeStruct((2 * rows, units), BF16),
        ]
        + [jax.ShapeDtypeStruct((units, 2 * rows), BF16)] * 3,
        compiler_params=pltpu.CompilerParams(vmem_limit_bytes=VMEM_LIMIT),
        cost_estimate=pl.CostEstimate(
            flops=20 * rows * model * units, bytes_accessed=30 << 20, transcendentals=2 << 20
        ),
        name="ffn",
    )(place, normed, normed_other, cot, cot_other, *blocks)


def ffn_out_kernel(pairs, half, place_ref, h_ref, *rest):
    blocks = rest[:-4]
    own_ref, other_ref, full_ref, sems = rest[-4:]

    @pl.when(pl.program_id(0) == 0)
    def _():
        all_copies = block_copies(place_ref, blocks, full_ref, sems, 2 * half, half, pairs)
        for copy in all_copies:
            copy.start()
        for copy in all_copies:
            copy.wait()

    out = matmul(h_ref[...], full_ref[...])
    mine = pl.program_id(0) < pl.num_programs(0) // 2

    @pl.when(mine)
    def _():
        own_ref[...] = out

    @pl.when(jnp.logical_not(mine))
    def _():
        other_ref[...] = out.astype(BF16)


def ffn_out(place, hidden, blocks, half, pairs, model):
    both, units = hidden.shape
    rows = both // 2
    step = 256
    each = rows // step
    own = pl.BlockSpec((step, model), lambda i, b: (jnp.minimum(i, each - 1), 0))
    other = pl.BlockSpec((step, model), lambda i, b: (jnp.maximum(i - each, 0), 0))
    return pl.pallas_call(
        functools.partial(ffn_out_kernel, pairs, half),
        grid_spec=pltpu.PrefetchScalarGridSpec(
            num_scalar_prefetch=1,
            grid=(2 * each,),
            in_specs=[pl.BlockSpec((step, units), lambda i, b: (i, 0))]
            + [pl.BlockSpec(memory_space=pl.ANY)] * len(blocks),
            out_specs=[own, other],
            scratch_shapes=[
                pltpu.VMEM((units, model), BF16), pltpu.SemaphoreType.DMA((len(blocks),)),
            ],
        ),
        out_shape=[
            jax.ShapeDtypeStruct((rows, model), F32), jax.ShapeDtypeStruct((rows, model), BF16),
        ],
        compiler_params=pltpu.CompilerParams(vmem_limit_bytes=VMEM_LIMIT),
        cost_estimate=pl.CostEstimate(
            flops=4 * rows * model * units, bytes_accessed=9 << 20, transcendentals=0
        ),
        name="ffn_out",
    )(place, hidden, *blocks)


def ffn_weights_kernel(half, col_ref, gt_ref, ut_ref, ht_ref, n0_ref, n1_ref, c0_ref, c1_ref, *outs):
    rows = n0_ref.shape[0]
    for which, (left, r0, r1) in enumerate(
        ((gt_ref, n0_ref, n1_ref), (ut_ref, n0_ref, n1_ref), (ht_ref, c0_ref, c1_ref))
    ):
        for ring, out in enumerate(outs):
            units = slice(ring * half, (ring + 1) * half)
            grad = matmul(left[units, :rows], r0[...]) + matmul(left[units, rows:], r1[...])
            out[which * half : (which + 1) * half, :] = grad.astype(BF16)


def ffn_weights(column, wide, half, grad_gate, grad_up, hidden, normed, normed_other, cot, cot_other):
    units, both = hidden.shape
    rows = both // 2
    whole = pl.BlockSpec((units, both), lambda i, c: (0, 0))
    block = pl.BlockSpec((rows, wide), lambda i, c: (0, c[0]))
    rings = units // half
    return pl.pallas_call(
        functools.partial(ffn_weights_kernel, half),
        grid_spec=pltpu.PrefetchScalarGridSpec(
            num_scalar_prefetch=1,
            grid=(1,),
            in_specs=[whole] * 3 + [block] * 4,
            out_specs=[pl.BlockSpec((3 * half, wide), lambda i, c: (0, 0))] * rings,
        ),
        out_shape=[jax.ShapeDtypeStruct((3 * half, wide), BF16)] * rings,
        compiler_params=pltpu.CompilerParams(vmem_limit_bytes=VMEM_LIMIT),
        cost_estimate=pl.CostEstimate(
            flops=6 * both * units * wide, bytes_accessed=13 << 20, transcendentals=0
        ),
        name="ffn_weights",
    )(column, grad_gate, grad_up, hidden, normed, normed_other, cot, cot_other)


def add_low(left, right):
    return (left.astype(F32) + right.astype(F32)).astype(BF16)


def on_device(
    hidden_in, value_first, segment_ids, gain_attn, w_query, w_key, w_value, w_out,
    gain_ffn, w_gate, w_up, w_down, cotangent, *, chips, depth,
):
    swap = lambda v: lax.ppermute(v, "core", [(0, 1), (1, 0)])
    onward = lambda v: lax.ppermute(v, "tensor", [(i, (i + 1) % depth) for i in range(depth)])
    across = lambda v, bit: lax.ppermute(v, "chip", [(i, i ^ bit) for i in range(chips)])
    rows, model = hidden_in.shape
    part = w_query.shape[0]
    units = w_gate.shape[1]
    half = units // 2
    heads_wide = w_query.shape[1]
    fast = chips == 4 and part == 128
    pairs = chips if fast else 1
    place = jnp.stack(
        [lax.axis_index("tensor"), lax.axis_index("chip"), lax.axis_index("core")]
    ).astype(jnp.int32)
    ring_block = lambda k: lax.rem(place[:1] + (depth - k), depth)

    x_parts = [hidden_in]
    for _ in range(depth - 1):
        x_parts.append(onward(x_parts[-1]))
    w_qkv = lax.all_gather(
        jnp.concatenate([w_query, w_key, w_value], axis=1), ("chip", "core"), axis=0, tiled=True
    )

    mlp_local = jnp.concatenate([w_gate.T, w_up.T, w_down]).reshape(3, 2, half, part)
    mlp_local = lax.all_to_all(mlp_local, "core", 1, 3, tiled=True).reshape(3 * half, 2 * part)
    if fast:
        out_local = jnp.concatenate([w_out[:part], w_out[part:]], axis=1)
        local = jnp.concatenate([mlp_local, out_local])
    else:
        local = lax.all_gather(mlp_local, "chip", axis=1, tiled=True)
    slots = [local]
    for _ in range(depth - 1):
        slots.append(onward(slots[-1]))
    if fast:
        blocks = []
        for k, slot in enumerate(slots):
            low, high = (1, 2) if k % 2 == 0 else (2, 1)
            near, far = across(slot, low), across(slot, high)
            group = {0: slot, low: near, high: far, 3: across(near, high)}
            blocks.extend(group[r] for r in range(4))
        mine = jnp.stack([b[3 * half :] for b in blocks]).reshape(depth, pairs, part, 2 * part)
        out_full = fill_out(place, mine, swap(mine))
    else:
        blocks = slots
        out_parts = lax.all_gather(w_out, ("chip", "core", "tensor"), axis=0)
        out_full = (
            out_parts.reshape(2 * chips, depth, heads_wide, part)
            .transpose(1, 2, 0, 3)
            .reshape(depth * heads_wide, model)
        )

    position = token_positions(segment_ids)
    cosine, sine = rotation_tables(position)
    seg_col, seg_row = segment_ids.reshape(-1, 1), segment_ids.reshape(1, -1)
    gain_one, gain_two = gain_attn.reshape(1, model), gain_ffn.reshape(1, model)
    filled = ()
    for k, x_part in enumerate(x_parts):
        filled = project(ring_block(k), filled, x_part, w_qkv, gain_one, cosine, sine, value_first)
    normed_all, query, key, value = filled
    mixed, lse = attend(query, key, value, seg_col, seg_row)
    attended = lax.all_to_all(mixed, "tensor", 0, 1, tiled=True)

    middle, normed = middle_rows(attended, out_full, hidden_in, gain_two)
    normed_other, cot_other = swap(normed), swap(cotangent)
    grad_own, grad_other, hidden, hidden_t, gate_t, up_t = ffn(
        place, normed, normed_other, cotangent, cot_other, blocks, half, pairs
    )
    grad_middle, grad_low, grad_att, gain_two_part = middle_back(
        grad_own, swap(grad_other), middle, cotangent, gain_two, out_full
    )
    grad_mixed = lax.all_to_all(grad_att, "tensor", 1, 0, tiled=True)

    out_own, out_other = ffn_out(place, hidden, blocks, half, pairs, model)
    output = (middle + out_own + swap(out_other).astype(F32)).astype(BF16)

    terms = {}
    for r in (3, 1, 2, 0) if fast else (0,):
        column = (place[1:2] ^ r) if fast else jnp.zeros((1,), jnp.int32)
        terms[r] = ffn_weights(
            column, model // pairs, half, gate_t, up_t, hidden_t,
            normed, normed_other, cotangent, cot_other,
        )
    sums = []
    for k in range(depth):
        if fast:
            low, high = (1, 2) if k % 2 == 0 else (2, 1)
            own = add_low(terms[low][k], across(terms[3][k], high))
            first = add_low(terms[0][k], across(terms[high][k], high))
            sums.append(add_low(first, across(own, low)))
        else:
            spread = terms[0][k].reshape(3 * half, chips, 2 * part).transpose(1, 0, 2)
            sums.append(lax.psum_scatter(spread, "chip", scatter_dimension=0))
    total = sums[1 % depth]
    for k in range(2, depth + 1):
        total = add_low(sums[k % depth], onward(total))
    mlp_sum = lax.all_to_all(
        total.reshape(3, 1, half, 2 * part), "core", 3, 1, tiled=True
    ).reshape(3, units, part).astype(F32)

    out_grad = (
        contract_rows(attended, grad_low)
        .astype(BF16)
        .reshape(depth * heads_wide, 2 * chips, part)
        .transpose(1, 0, 2)
    )
    out_sum = lax.psum_scatter(
        lax.psum_scatter(out_grad, ("chip", "core"), scatter_dimension=0),
        "tensor",
        scatter_dimension=0,
        tiled=True,
    )

    qkv_grads, grad_value_first = attend_back(
        query, key, value, grad_mixed, mixed, lse, seg_col, seg_row, cosine, sine
    )
    arrived, gain_one_part = None, 0.0
    for k in range(1, depth + 1):
        final = grad_middle if k == depth else None
        back, gain_term = unproject(
            ring_block(k % depth), qkv_grads, w_qkv, x_parts[k % depth], gain_one, arrived, final
        )
        gain_one_part = gain_one_part + gain_term
        if k < depth:
            arrived = onward(back)
    grad_input = back
    qkv_sum = lax.psum_scatter(
        contract_rows(normed_all, qkv_grads).astype(BF16),
        ("chip", "core"),
        scatter_dimension=0,
        tiled=True,
    ).astype(F32)
    devices = 2 * chips * depth
    gains = jnp.concatenate([gain_one_part, gain_two_part]).reshape(2, devices, -1).transpose(1, 0, 2)
    gains = jnp.sum(
        lax.all_to_all(gains, ("chip", "core", "tensor"), 0, 0, tiled=True), axis=0
    )
    return (
        output,
        grad_input,
        grad_value_first,
        gains[0],
        qkv_sum[:, :heads_wide],
        qkv_sum[:, heads_wide : 2 * heads_wide],
        qkv_sum[:, 2 * heads_wide :],
        out_sum.astype(F32),
        gains[1],
        mlp_sum[0].T,
        mlp_sum[1].T,
        mlp_sum[2],
    )


def solution(mesh):
    dp, depth = mesh.shape["dp"], mesh.shape["tensor"]
    chips = dp // 2
    fine = Mesh(mesh.devices.reshape(chips, 2, depth), ("chip", "core", "tensor"))
    every = ("chip", "core", "tensor")
    split = ("chip", "core")
    return jax.shard_map(
        functools.partial(on_device, chips=chips, depth=depth),
        mesh=fine,
        in_specs=(
            P(every, None), P(split, "tensor"), P(split), P(),
            P(split, "tensor"), P(split, "tensor"), P(split, "tensor"), P("tensor", split),
            P(), P(split, "tensor"), P(split, "tensor"), P("tensor", split), P(every, None),
        ),
        out_specs=(
            P(every, None), P(every, None), P(split, "tensor"), P(every),
            P(split, "tensor"), P(split, "tensor"), P(split, "tensor"), P("tensor", split),
            P(every), P(split, "tensor"), P(split, "tensor"), P("tensor", split),
        ),
        check_vma=False,
    )
```
